32 devices in a mesh: grp: 2 (over x), seq: 16 (over z, y, core).
Axes of the slice: x: 2, y: 2, z: 4, core: 2. Of those that a mesh axis runs over, the one named last changes fastest.
Arguments:
- hidden: bfloat16 [16384, 4096], P(('grp', 'seq')), parts along dimension 0, may hold values from -6 to 6
- token_ids: int32 [32, 512], P(('grp', 'seq')), parts along dimension 0, may hold values from 0 to 128255, as said below
- upstream: bfloat16 [16384, 1024], P(('grp', 'seq')), parts along dimension 0, may hold values from -6 to 6
- w_value: bfloat16 [4096, 1024], P('seq'), may hold values from -0.09375 to 0.09375
- proj_in: bfloat16 [4096, 64], replicated, may hold values from -0.09375 to 0.09375
- proj_out: bfloat16 [8, 128, 64], replicated, may hold values from -0.5 to 0.5
- in_inverse: float32 [8, 64, 64], replicated
- out_inverse: float32 [8, 64, 64], replicated
- datastore: bfloat16 [1024, 32768], P(('grp', 'seq')), parts along dimension 0
Outputs:
- input_grad: bfloat16 [16384, 4096], P(('grp', 'seq')), parts along dimension 0
- scores: float32 [32, 512], P('grp', 'seq'), parts along dimension 0
The draws below stay inside these ranges and needn't reach their ends.
There are 2 independent parts, one for each index of `grp`. The reference program is written for one: setup_inputs(seed, part) draws one part's arguments, and reference() takes and returns one part's arrays. A program takes and returns all parts, laid end to end along the dimension named above; an argument that names none is the same for every part. Nothing has to cross between parts.
Inputs may be any that keep to these rules, and one draw needn't show every extreme that they name: `token_ids`: each sequence holds its live tokens first, then padding ids 0; at least 128 tokens of every sequence are live and some sequence has no padding.
All inputs are finite; a program needn't handle non-finite values.
Results may differ from the reference program's by a relative error of at most 0.0059.
Values may be sent and summed in bfloat16 or wider, within the bound.
A program may use at most 128 MiB of HBM per device.

```python
import jax
import jax.numpy as jnp
from jax import lax

D = 4096
KVH = 8
HD = 128
RANK = 64
TOK = 512
KV = 1024
FLAT = 32768
QUERIES = 16
DS_ROWS = 512


def draw_token_ids(key, part):
    key_len = jax.random.fold_in(key, 11)
    key_ids = jax.random.fold_in(key, 12)
    key_full = jax.random.fold_in(key, 13)
    lengths = jax.random.randint(key_len, (QUERIES,), TOK // 4, TOK + 1)
    full_row = jax.random.randint(key_full, (), 0, QUERIES)
    lengths = lengths.at[full_row].set(TOK)
    ids_drawn = jax.random.randint(key_ids, (QUERIES, TOK), 1, 128256)
    ids_drawn = ids_drawn.at[full_row, 0].set(128255)
    position = jnp.arange(TOK, dtype=jnp.int32)[None, :]
    return jnp.where(position < lengths[:, None], ids_drawn, 0).astype(jnp.int32)


def inverse_factor(key):
    key_diag = jax.random.fold_in(key, 21)
    key_off = jax.random.fold_in(key, 22)
    diag_vals = jax.random.uniform(key_diag, (KVH, RANK), jnp.float32, 1.0, 2.0)
    noise = jax.random.normal(key_off, (KVH, RANK, RANK), jnp.float32)
    noise = 0.5 * (noise + jnp.swapaxes(noise, 1, 2)) / jnp.sqrt(2.0 * RANK)
    eye_mat = jnp.eye(RANK, dtype=jnp.float32)[None]
    return eye_mat * diag_vals[:, :, None] + noise


def draw_in_inverse(key, part):
    return inverse_factor(jax.random.fold_in(key, 31))


def draw_out_inverse(key, part):
    return inverse_factor(jax.random.fold_in(key, 32))


def draw_datastore(key, part):
    key_val = jax.random.fold_in(key, 41)
    key_row = jax.random.fold_in(key, 42)
    row_pos = jnp.arange(DS_ROWS, dtype=jnp.float32) / DS_ROWS
    row_scale = jnp.exp(jax.random.uniform(key_row, (DS_ROWS,), jnp.float32, 0.0, 2.3026)) * jnp.exp(1.0986 * row_pos)
    values = jax.random.normal(key_val, (DS_ROWS, FLAT), jnp.float32)
    return (values * row_scale[:, None]).astype(jnp.bfloat16)


def block_levels(key, extent, shards, smallest, top_value):
    loudness = 1.0
    for dim, shards_of in shards:
        steps = jax.random.uniform(jax.random.fold_in(jax.random.fold_in(key, 6), dim), (shards_of,), jnp.float32, smallest / len(shards), top_value / len(shards))
        loudness = loudness * jnp.repeat(jnp.exp(steps), extent[dim] // shards_of).reshape((-1,) + (1,) * (len(extent) - 1 - dim))
    return loudness


def scatter_about(own_key, shape, scale, most, split=(), held_as=jnp.bfloat16):
    factor_of = block_levels(own_key, shape, split, -0.22, 0.18) if split else 1.0
    values = jax.random.normal(own_key, shape, jnp.float32) * scale * factor_of
    return jnp.minimum(jnp.maximum(values, -most), most).astype(held_as)


def setup_inputs(seed: int = 0, part: int = 0) -> dict:
    streams_of = jax.random.split(jax.random.key(seed), 10)
    part_splits = jax.random.split(jax.random.fold_in(streams_of[9], part), 10)
    return {
        "hidden": scatter_about(part_splits[0], (QUERIES * TOK, D), 1.0, 6.0, ((0, 16),)),
        "token_ids": draw_token_ids(jax.random.fold_in(jax.random.fold_in(streams_of[9], part), 71), part),
        "upstream": scatter_about(part_splits[2], (QUERIES * TOK, KV), 1.0, 6.0, ((0, 16),)),
        "w_value": scatter_about(streams_of[3], (D, KV), D ** -0.5, 0.09375, ((0, 16),)),
        "proj_in": scatter_about(streams_of[4], (D, RANK), D ** -0.5, 0.09375),
        "proj_out": scatter_about(streams_of[5], (KVH, HD, RANK), HD ** -0.5, 0.5),
        "in_inverse": draw_in_inverse(jax.random.fold_in(streams_of[9], 71), part),
        "out_inverse": draw_out_inverse(jax.random.fold_in(streams_of[9], 71), part),
        "datastore": draw_datastore(jax.random.fold_in(jax.random.fold_in(streams_of[9], part), 71), part),
    }


def reference(hidden, token_ids, upstream, w_value, proj_in, proj_out, in_inverse, out_inverse, datastore):
    live_mask = (token_ids != 0).reshape(-1, 1).astype(jnp.bfloat16)
    masked = upstream * live_mask
    input_grad = jnp.dot(masked, w_value.T, preferred_element_type=jnp.float32).astype(jnp.bfloat16)
    left_proj = jnp.dot(hidden, proj_in, preferred_element_type=jnp.float32).astype(jnp.bfloat16)
    cot_heads = masked.reshape(-1, KVH, HD).astype(jnp.float32)
    right_proj = jnp.einsum('thd,hdr->thr', cot_heads, proj_out.astype(jnp.float32)).astype(jnp.bfloat16)
    left_seq = left_proj.astype(jnp.float32).reshape(QUERIES, TOK, RANK)
    right_seq = right_proj.astype(jnp.float32).reshape(QUERIES, TOK, KVH, RANK)
    raw_grads = jnp.einsum('qti,qthj->qhij', left_seq, right_seq)
    half_way = jnp.einsum('hai,qhij->qhaj', in_inverse, raw_grads, precision=lax.Precision.HIGHEST)
    pre_grads = jnp.einsum('qhaj,hjb->qhab', half_way, out_inverse, precision=lax.Precision.HIGHEST)
    query_grads = pre_grads.astype(jnp.bfloat16).reshape(QUERIES, FLAT)
    raw_scores = jnp.dot(query_grads, datastore.T, preferred_element_type=jnp.float32)
    spread = jnp.sqrt(lax.optimization_barrier(jnp.mean(raw_scores * raw_scores, axis=1, keepdims=True)) + 1e-06)
    return (input_grad, raw_scores / spread)
```

```python
import functools

import jax
import jax.numpy as jnp
from jax import lax
from jax.experimental import pallas as pl
from jax.experimental.pallas import tpu as pltpu
from jax.sharding import PartitionSpec as P

CORES = 2
LANES = 128
HID_CHUNKS = 4
MESH = pl.DeviceIdType.MESH


def ring_shape(chips):
    fast = 1
    while fast * fast * 4 <= chips:
        fast *= 2
    return chips // fast, fast


def chip_at(pos, chips):
    rows, cols = ring_shape(chips)
    snake = rows * (cols - 1)
    r1 = pos // (cols - 1)
    k1 = pos % (cols - 1)
    c1 = jnp.where(r1 % 2 == 0, 1 + k1, cols - 1 - k1)
    r2 = rows - 1 - (pos - snake)
    inside = pos < snake
    return jnp.where(inside, r1 * cols + c1, r2 * cols)


def pos_of(chip, chips):
    rows, cols = ring_shape(chips)
    snake = rows * (cols - 1)
    r, c = chip // cols, chip % cols
    k = jnp.where(r % 2 == 0, c - 1, cols - 1 - c)
    return jnp.where(c == 0, snake + rows - 1 - r, r * (cols - 1) + k)


def kernel(
    groups, members, across,
    tok_h, hid_h, up_h, w_h, pin_h, pout_h, ain_h, bout_h, ds_h,
    out, sc,
    wf, hid, up, tok, pin, pout, ain, bout, ds, left_s, qall, qtmp, qmat, pw,
    load_sem, hid_sem, own_sem,
    ws, wr, xs, xr, ds1, dr1, ds2, dr2, dos, dor,
    qs, qr, qds, qdr, qos, qor, ps, pr,
):
    chips = members // CORES
    half = chips // 2
    shard = w_h.shape[0]
    heads, head_dim, rank = pout_h.shape
    ring = shard - across
    g = lax.axis_index("grp")
    me = lax.axis_index("seq")
    core = me % CORES
    pos = pos_of(me // CORES, chips)
    mate = me + 1 - 2 * core

    def index(p, c):
        return chip_at((p + 2 * chips) % chips, chips) * CORES + c

    nxt = index(pos + 1, core)
    prv = index(pos - 1, core)
    sends = (nxt, prv)

    def origin(d, s, c):
        return index(pos - s if d == 0 else pos + s, c)

    def remote(src, dst, ssem, rsem, where):
        return pltpu.make_async_remote_copy(
            src_ref=src, dst_ref=dst, send_sem=ssem, recv_sem=rsem,
            device_id=where, device_id_type=MESH)

    loads = []

    def load(src, dst, sem):
        copy = pltpu.make_async_copy(src, dst, sem)
        loads.append(copy)
        return copy

    c_w = load(w_h, wf.at[me], own_sem)
    c_tok = load(tok_h, tok, load_sem.at[0])
    c_up = load(up_h, up, load_sem.at[1])
    c_pin = load(pin_h, pin, load_sem.at[2])
    c_pout = load(pout_h, pout, load_sem.at[3])
    c_ain = load(ain_h, ain, load_sem.at[4])
    c_bout = load(bout_h, bout, load_sem.at[5])
    c_ds = load(ds_h, ds, load_sem.at[6])
    tokens = hid_h.shape[0]
    part = tokens // HID_CHUNKS
    c_hid = [load(hid_h.at[pl.ds(i * part, part)], hid.at[pl.ds(i * part, part)], hid_sem.at[i])
             for i in range(HID_CHUNKS)]
    for copy in (c_w, c_tok, c_up, c_pin, *c_hid, c_pout, c_ain, c_bout, c_ds):
        copy.start()

    barrier = pltpu.get_barrier_semaphore()

    def greet(j, carry):
        pl.semaphore_signal(barrier, inc=1, device_id={"seq": (me + j) % members}, device_id_type=MESH)
        return carry

    lax.fori_loop(1, members, greet, 0)
    greeted = members - 1
    if across:
        pl.semaphore_signal(barrier, inc=1, device_id={"grp": 1 - g}, device_id_type=MESH)
        greeted += 1
    pl.semaphore_wait(barrier, greeted)

    ring_off = pl.multiple_of(g * across, 16)
    half_off = pl.multiple_of(g * across + ring // 2, 16)
    x_out = pl.multiple_of(g * ring, 16)
    x_in = pl.multiple_of((1 - g) * ring, 16)

    def rows(o, off, n):
        return wf.at[o, pl.ds(off, n)]

    def hop(d, s, last, recv=False):
        o = origin(d, s if recv else s - 1, core)
        off = half_off if last and d == 1 else ring_off
        ref = rows(o, off, ring // 2 if last else ring)
        return remote(ref, ref, ws.at[d, s], wr.at[d, s], {"seq": sends[d]})

    def cross(d, s, recv=False):
        ref = rows(origin(d, s, core), x_in if recv else x_out, across)
        return remote(ref, ref, xs.at[d, s], xr.at[d, s], {"grp": 1 - g})

    def side_ring(d, s, recv=False):
        ref = rows(origin(d, s, 1 - core if recv else core), ring_off, ring)
        return remote(ref, ref, ds1.at[d, s], dr1.at[d, s], {"seq": mate})

    def side_cross(d, s, recv=False):
        ref = rows(origin(d, s, 1 - core if recv else core), x_in, across)
        return remote(ref, ref, ds2.at[d, s], dr2.at[d, s], {"seq": mate})

    def side_own(recv=False):
        ref = wf.at[mate if recv else me]
        return remote(ref, ref, dos, dor, {"seq": mate})

    def q_hop(d, s, recv=False):
        ref = qall.at[origin(d, s if recv else s - 1, core)]
        return remote(ref, ref, qs.at[d, s], qr.at[d, s], {"seq": sends[d]})

    def q_side(d, s, recv=False):
        ref = qall.at[origin(d, s, 1 - core if recv else core)]
        return remote(ref, ref, qds.at[d, s], qdr.at[d, s], {"seq": mate})

    def q_own(recv=False):
        ref = qall.at[mate if recv else me]
        return remote(ref, ref, qos, qor, {"seq": mate})

    c_w.wait()
    for d in range(2):
        hop(d, 1, False).start()
    side_own().start()

    c_tok.wait()
    c_up.wait()
    live = jnp.sum((tok[...] != 0).astype(jnp.float32), axis=1, keepdims=True)
    place = lax.broadcasted_iota(jnp.int32, (tokens, 1), 0).astype(jnp.float32)
    keep = place < live
    up[...] = jnp.where(keep, up[...], jnp.zeros_like(up))
    c_pin.wait()
    for i in range(HID_CHUNKS):
        c_hid[i].wait()
        left_s[pl.ds(i * part, part), :] = jnp.dot(
            hid[pl.ds(i * part, part), :], pin[...], preferred_element_type=jnp.float32
        ).astype(jnp.bfloat16)
    c_pout.wait()
    c_ain.wait()
    c_bout.wait()
    left_t = left_s[...].T
    for h in range(heads):
        right = jnp.dot(
            up[:, h * head_dim:(h + 1) * head_dim], pout[h], preferred_element_type=jnp.float32
        ).astype(jnp.bfloat16)
        raw = jnp.dot(left_t, right, preferred_element_type=jnp.float32)
        inv = jnp.concatenate(
            [ain[h, pl.ds(0, rank // 2, stride=2), :], ain[h, pl.ds(1, rank // 2, stride=2), :]], axis=0)
        first = jnp.dot(inv, raw, precision=lax.Precision.HIGHEST, preferred_element_type=jnp.float32)
        both = jnp.dot(first, bout[h], precision=lax.Precision.HIGHEST, preferred_element_type=jnp.float32)
        flat = jnp.concatenate([both[:rank // 2], both[rank // 2:]], axis=1)
        qall[me, pl.ds(h * rank // 2, rank // 2), :] = flat.astype(jnp.bfloat16)

    for d in range(2):
        q_hop(d, 1).start()
    q_own().start()

    aligned = shard % LANES == 0

    def multiply(o):
        cols = pl.ds(pl.multiple_of(o * shard, LANES), shard)
        out[:, cols] = lax.dot_general(
            up[...], wf[o], (((1,), (1,)), ((), ())), preferred_element_type=jnp.float32
        ).astype(jnp.bfloat16)

    def own_pair(s):
        if aligned:
            def body(d, carry):
                multiply(index(pos + (2 * d - 1) * s, core))
                return carry
            lax.fori_loop(0, 2, body, 0)

    def mate_pair(s):
        for d in range(2):
            side_ring(d, s, True).wait_recv()
            if across:
                side_cross(d, s, True).wait_recv()
        if aligned:
            def body(d, carry):
                multiply(index(pos + (2 * d - 1) * s, 1 - core))
                return carry
            lax.fori_loop(0, 2, body, 0)

    def cross_pair(s):
        if across:
            for d in range(2):
                cross(d, s, True).wait_recv()
                side_cross(d, s).start()

    side_own(True).wait_recv()
    if aligned:
        def body(d, carry):
            multiply(me + d * (1 - 2 * core))
            return carry
        lax.fori_loop(0, 2, body, 0)

    def step(s, carry):
        for d in range(2):
            q_hop(d, s, True).wait_recv()
            if d == 0:
                q_hop(d, s + 1).start()
            else:
                @pl.when(s < half - 1)
                def _():
                    q_hop(1, s + 1).start()
            q_side(d, s).start()
        for d in range(2):
            hop(d, s, False, True).wait_recv()

            @pl.when(s < half - 1)
            def _():
                hop(d, s + 1, False).start()

            @pl.when(s == half - 1)
            def _():
                hop(d, s + 1, True).start()

            if across:
                cross(d, s).start()
            side_ring(d, s).start()

        @pl.when(s >= 2)
        def _():
            cross_pair(s - 1)
            own_pair(s - 1)

        @pl.when(s >= 3)
        def _():
            mate_pair(s - 2)
        return carry

    lax.fori_loop(1, half, step, 0)

    q_hop(0, half, True).wait_recv()
    q_side(0, half).start()
    q_own(True).wait_recv()

    def q_wait(s, carry):
        for d in range(2):
            q_side(d, s, True).wait_recv()
        return carry

    lax.fori_loop(1, half, q_wait, 0)
    cross_pair(half - 1)
    own_pair(half - 1)
    q_side(0, half, True).wait_recv()

    c_ds.wait()
    block = qtmp.shape[1]

    def unfold(b, carry):
        qtmp[...] = qall[:, pl.ds(pl.multiple_of(b * block, block), block), :].astype(jnp.float32)
        flat_ref = qtmp.reshape(members * block, LANES)
        for k in range(block):
            piece = flat_ref[pl.ds(k, members, stride=block), :]
            qmat[:, pl.ds(pl.multiple_of((b * block + k) * LANES, LANES), LANES)] = piece.astype(jnp.bfloat16)
        return carry

    lax.fori_loop(0, qall.shape[1] // block, unfold, 0)
    flat_len = qmat.shape[1]
    wide = min(flat_len, 8192)

    def score(b, total):
        cols = pl.ds(pl.multiple_of(b * wide, wide), wide)
        return total + lax.dot_general(
            qmat[:, cols], ds[:, cols], (((1,), (1,)), ((), ())), preferred_element_type=jnp.float32)

    scores = lax.fori_loop(0, flat_len // wide, score, jnp.zeros(sc.shape, jnp.float32))
    sc[...] = scores
    power = jnp.sum(scores * scores, axis=1, keepdims=True)
    lane_width = pw.shape[2]
    eye = (lax.broadcasted_iota(jnp.int32, (members, lane_width), 0)
           == lax.broadcasted_iota(jnp.int32, (members, lane_width), 1))
    pw[me] = jnp.sum(jnp.where(eye, power, 0.0), axis=0, keepdims=True)

    def p_copy(j, recv=False):
        ref = pw.at[(me - j + members) % members if recv else me]
        return remote(ref, ref, ps.at[j], pr.at[j], {"seq": (me + j) % members})

    def p_start(j, carry):
        p_copy(j).start()
        return carry

    lax.fori_loop(1, members, p_start, 0)

    for d in range(2):
        hop(d, half, True, True).wait_recv()
    if across:
        cross(0, half).start()
    side_ring(0, half).start()
    if half >= 3:
        mate_pair(half - 2)
    mate_pair(half - 1)
    if across:
        cross(0, half, True).wait_recv()
        side_cross(0, half).start()
    if aligned:
        multiply(index(pos + half, core))
    side_ring(0, half, True).wait_recv()
    if across:
        side_cross(0, half, True).wait_recv()
    if aligned:
        multiply(index(pos + half, 1 - core))
    else:
        def big(b, carry):
            per = LANES // shard
            weights = wf[pl.ds(b * per, per)].reshape(LANES, wf.shape[2])
            out[:, pl.ds(pl.multiple_of(b * LANES, LANES), LANES)] = lax.dot_general(
                up[...], weights, (((1,), (1,)), ((), ())), preferred_element_type=jnp.float32
            ).astype(jnp.bfloat16)
            return carry
        lax.fori_loop(0, members * shard // LANES, big, 0)

    def p_wait(j, carry):
        p_copy(j, True).wait_recv()
        return carry

    lax.fori_loop(1, members, p_wait, 0)
    summed = jnp.sum(pw[...], axis=0)
    column = jnp.sum(jnp.where(eye, summed, 0.0), axis=1, keepdims=True)
    spread = jnp.sqrt(column / (ds_h.shape[0] * members) + 1e-06)
    sc[...] = sc[...] / spread

    side_own().wait_send()
    q_own().wait_send()

    def sent(s, carry):
        for d in range(2):
            q_hop(d, s).wait_send()
            q_side(d, s).wait_send()
            hop(d, s, False).wait_send()
            side_ring(d, s).wait_send()
            if across:
                cross(d, s).wait_send()
                side_cross(d, s).wait_send()
        return carry

    lax.fori_loop(1, half, sent, 0)
    q_hop(0, half).wait_send()
    q_side(0, half).wait_send()
    for d in range(2):
        hop(d, half, True).wait_send()
    side_ring(0, half).wait_send()
    if across:
        cross(0, half).wait_send()
        side_cross(0, half).wait_send()

    def p_sent(j, carry):
        p_copy(j).wait_send()
        return carry

    lax.fori_loop(1, members, p_sent, 0)


def on_device(groups, members, *args):
    hidden, token_ids, upstream, w_value, proj_in, proj_out, in_inverse, out_inverse, datastore = args
    shard, width = w_value.shape
    tokens, model = hidden.shape
    assert token_ids.shape[0] == 1 and members % (2 * CORES) == 0
    flat = datastore.shape[1]
    across = 0
    if groups == 2:
        across = shard * 3 // 8 // 32 * 32
    half = members // CORES // 2
    steps = half + 1
    dma = pltpu.SemaphoreType.DMA
    lane_width = max(LANES, members)
    anywhere = pl.BlockSpec(memory_space=pl.ANY)
    vmem = pl.BlockSpec(memory_space=pltpu.VMEM)
    bf = jnp.bfloat16
    return pl.pallas_call(
        functools.partial(kernel, groups, members, across),
        out_shape=(
            jax.ShapeDtypeStruct((tokens, members * shard), bf),
            jax.ShapeDtypeStruct((members, datastore.shape[0]), jnp.float32),
        ),
        in_specs=[anywhere, anywhere, anywhere, anywhere, anywhere, anywhere, anywhere, anywhere, anywhere],
        out_specs=(vmem, vmem),
        scratch_shapes=[
            pltpu.VMEM((members, shard, width), bf),
            pltpu.VMEM((tokens, model), bf),
            pltpu.VMEM((tokens, width), bf),
            pltpu.VMEM(token_ids.shape, jnp.int32),
            pltpu.VMEM(proj_in.shape, bf),
            pltpu.VMEM(proj_out.shape, bf),
            pltpu.VMEM(in_inverse.shape, jnp.float32),
            pltpu.VMEM(out_inverse.shape, jnp.float32),
            pltpu.VMEM(datastore.shape, bf),
            pltpu.VMEM((tokens, proj_in.shape[1]), bf),
            pltpu.VMEM((members, flat // LANES, LANES), bf),
            pltpu.VMEM((members, 16, LANES), jnp.float32),
            pltpu.VMEM((members, flat), bf),
            pltpu.VMEM((members, 1, lane_width), jnp.float32),
            dma((7,)), dma((HID_CHUNKS,)), dma,
            dma((2, steps)), dma((2, steps)), dma((2, steps)), dma((2, steps)),
            dma((2, steps)), dma((2, steps)), dma((2, steps)), dma((2, steps)), dma, dma,
            dma((2, steps)), dma((2, steps)), dma((2, steps)), dma((2, steps)), dma, dma,
            dma((members,)), dma((members,)),
        ],
        compiler_params=pltpu.CompilerParams(
            collective_id=0, has_side_effects=True, vmem_limit_bytes=60000 * 1024),
    )(token_ids, hidden, upstream, w_value, proj_in, proj_out, in_inverse, out_inverse, datastore)


def solution(mesh):
    rows = P(("grp", "seq"), None)
    placed = (rows, rows, rows, P("seq", None), P(), P(), P(), P(), rows)
    return jax.shard_map(
        functools.partial(on_device, mesh.shape["grp"], mesh.shape["seq"]),
        mesh=mesh,
        in_specs=placed,
        out_specs=(rows, P("grp", "seq")),
        check_vma=False,
    )
```

```python
import functools

import jax
import jax.numpy as jnp
from jax import lax
from jax.experimental import pallas as pl
from jax.experimental.pallas import tpu as pltpu
from jax.sharding import PartitionSpec as P

CORES = 2
LANES = 128
HID_CHUNKS = 4
MESH = pl.DeviceIdType.MESH


def ring_shape(chips):
    fast = 1
    while fast * fast * 4 <= chips:
        fast *= 2
    return chips // fast, fast


def chip_at(pos, chips):
    rows, cols = ring_shape(chips)
    snake = rows * (cols - 1)
    r1 = pos // (cols - 1)
    k1 = pos % (cols - 1)
    c1 = jnp.where(r1 % 2 == 0, 1 + k1, cols - 1 - k1)
    r2 = rows - 1 - (pos - snake)
    inside = pos < snake
    return jnp.where(inside, r1 * cols + c1, r2 * cols)


def pos_of(chip, chips):
    rows, cols = ring_shape(chips)
    snake = rows * (cols - 1)
    r, c = chip // cols, chip % cols
    k = jnp.where(r % 2 == 0, c - 1, cols - 1 - c)
    return jnp.where(c == 0, snake + rows - 1 - r, r * (cols - 1) + k)


def kernel(
    groups, members, across,
    tok_h, hid_h, up_h, w_h, pin_h, pout_h, ain_h, bout_h, ds_h,
    out, sc,
    wf, hid, up, tok, pin, pout, ain, bout, ds, left_s, qall, qtmp, qmat, pw,
    load_sem, hid_sem, own_sem,
    ws, wr, xs, xr, ds1, dr1, ds2, dr2, es, er, dls, dlr, dos, dor,
    qs, qr, qds, qdr, qos, qor, ps, pr,
):
    chips = members // CORES
    half = chips // 2
    shard = w_h.shape[0]
    heads, rank, head_dim = pout_h.shape
    piece = shard // 2
    ring = piece - across
    g = lax.axis_index("grp")
    me = lax.axis_index("seq")
    core = me % CORES
    pos = pos_of(me // CORES, chips)
    mate = me + 1 - 2 * core

    def index(p, c):
        return chip_at((p + 2 * chips) % chips, chips) * CORES + c

    nxt = index(pos + 1, core)
    prv = index(pos - 1, core)
    sends = (nxt, prv)

    def origin(d, s, c):
        return index(pos - s if d == 0 else pos + s, c)

    def remote(src, dst, ssem, rsem, where):
        return pltpu.make_async_remote_copy(
            src_ref=src, dst_ref=dst, send_sem=ssem, recv_sem=rsem,
            device_id=where, device_id_type=MESH)

    loads = []

    def load(src, dst, sem):
        copy = pltpu.make_async_copy(src, dst, sem)
        loads.append(copy)
        return copy

    c_w = load(w_h, wf.at[me], own_sem)
    c_tok = load(tok_h, tok, load_sem.at[0])
    c_up = load(up_h, up, load_sem.at[1])
    c_pin = load(pin_h, pin, load_sem.at[2])
    c_pout = load(pout_h, pout, load_sem.at[3])
    c_ain = load(ain_h, ain, load_sem.at[4])
    c_bout = load(bout_h, bout, load_sem.at[5])
    c_ds = load(ds_h, ds, load_sem.at[6])
    tokens = hid_h.shape[0]
    part = tokens // HID_CHUNKS
    c_hid = [load(hid_h.at[pl.ds(i * part, part)], hid.at[pl.ds(i * part, part)], hid_sem.at[i])
             for i in range(HID_CHUNKS)]
    for copy in (c_w, c_tok, c_up, c_pin, *c_hid, c_pout, c_ain, c_bout, c_ds):
        copy.start()

    barrier = pltpu.get_barrier_semaphore()

    def greet(j, carry):
        pl.semaphore_signal(barrier, inc=1, device_id={"seq": (me + j) % members}, device_id_type=MESH)
        return carry

    lax.fori_loop(1, members, greet, 0)
    greeted = members - 1
    if across:
        pl.semaphore_signal(barrier, inc=1, device_id={"grp": 1 - g}, device_id_type=MESH)
        greeted += 1
    pl.semaphore_wait(barrier, greeted)

    def rows(o, k, off, n):
        return wf.at[o, pl.ds(pl.multiple_of(k * piece + off, 16), n)]

    ring_off = g * across
    x_out = g * ring
    x_in = (1 - g) * ring

    def hop(d, s, k, recv=False):
        ref = rows(origin(d, s if recv else s - 1, core), k, ring_off, ring)
        return remote(ref, ref, ws.at[d, s, k], wr.at[d, s, k], {"seq": sends[d]})

    def extra(d, recv=False):
        ref = rows(origin(d, half if recv else half - 1, core), d, x_in, across)
        return remote(ref, ref, es.at[d], er.at[d], {"seq": sends[d]})

    def cross(d, s, k, recv=False):
        ref = rows(origin(d, s, core), k, x_in if recv else x_out, across)
        return remote(ref, ref, xs.at[d, s, k], xr.at[d, s, k], {"grp": 1 - g})

    def side_ring(d, s, k, recv=False):
        ref = rows(origin(d, s, 1 - core if recv else core), k, ring_off, ring)
        return remote(ref, ref, ds1.at[d, s, k], dr1.at[d, s, k], {"seq": mate})

    def side_cross(d, s, k, recv=False):
        ref = rows(origin(d, s, 1 - core if recv else core), k, x_in, across)
        return remote(ref, ref, ds2.at[d, s, k], dr2.at[d, s, k], {"seq": mate})

    def side_last(d, recv=False):
        ref = rows(origin(d, half, 1 - core if recv else core), d, 0, piece)
        return remote(ref, ref, dls.at[d], dlr.at[d], {"seq": mate})

    def side_own(recv=False):
        ref = wf.at[mate if recv else me]
        return remote(ref, ref, dos, dor, {"seq": mate})

    def q_hop(d, s, recv=False):
        ref = qall.at[origin(d, s if recv else s - 1, core)]
        return remote(ref, ref, qs.at[d, s], qr.at[d, s], {"seq": sends[d]})

    def q_side(d, s, recv=False):
        ref = qall.at[origin(d, s, 1 - core if recv else core)]
        return remote(ref, ref, qds.at[d, s], qdr.at[d, s], {"seq": mate})

    def q_own(recv=False):
        ref = qall.at[mate if recv else me]
        return remote(ref, ref, qos, qor, {"seq": mate})

    c_w.wait()
    for k in range(2):
        for d in range(2):
            hop(d, 1, k).start()
    side_own().start()

    def forward(s, k):
        for d in range(2):
            hop(d, s, k, True).wait_recv()
            if k == d:
                hop(d, s + 1, k).start()
            else:
                @pl.when(s < half - 1)
                def _():
                    hop(d, s + 1, k).start()
            if across:
                cross(d, s, k).start()
            side_ring(d, s, k).start()

    c_tok.wait()
    c_up.wait()
    live = jnp.sum((tok[...] != 0).astype(jnp.float32), axis=1, keepdims=True)
    place = lax.broadcasted_iota(jnp.int32, (tokens, 1), 0).astype(jnp.float32)
    keep = place < live
    up[...] = jnp.where(keep, up[...], jnp.zeros_like(up))
    c_pin.wait()
    for i in range(HID_CHUNKS):
        c_hid[i].wait()
        left_s[pl.ds(i * part, part), :] = lax.dot_general(
            hid[pl.ds(i * part, part), :], pin[...], (((1,), (1,)), ((), ())), preferred_element_type=jnp.float32
        ).astype(jnp.bfloat16)
    forward(1, 0)
    c_pout.wait()
    c_ain.wait()
    c_bout.wait()
    left_t = left_s[...].T
    for h in range(heads):
        right = lax.dot_general(
            up[:, h * head_dim:(h + 1) * head_dim], pout[h], (((1,), (1,)), ((), ())),
            preferred_element_type=jnp.float32
        ).astype(jnp.bfloat16)
        raw = jnp.dot(left_t, right, preferred_element_type=jnp.float32)
        inv = jnp.concatenate(
            [ain[h, pl.ds(0, rank // 2, stride=2), :], ain[h, pl.ds(1, rank // 2, stride=2), :]], axis=0)
        first = jnp.dot(inv, raw, precision=lax.Precision.HIGHEST, preferred_element_type=jnp.float32)
        both = jnp.dot(first, bout[h], precision=lax.Precision.HIGHEST, preferred_element_type=jnp.float32)
        flat = jnp.concatenate([both[:rank // 2], both[rank // 2:]], axis=1)
        qall[me, pl.ds(h * rank // 2, rank // 2), :] = flat.astype(jnp.bfloat16)

    for d in range(2):
        q_hop(d, 1).start()
    q_own().start()
    forward(1, 1)

    aligned = shard % LANES == 0

    def multiply(o):
        cols = pl.ds(pl.multiple_of(o * shard, LANES), shard)
        out[:, cols] = lax.dot_general(
            up[...], wf[o], (((1,), (1,)), ((), ())), preferred_element_type=jnp.float32
        ).astype(jnp.bfloat16)

    def own_pair(s):
        if aligned:
            def body(d, carry):
                multiply(index(pos + (2 * d - 1) * s, core))
                return carry
            lax.fori_loop(0, 2, body, 0)

    def mate_pair(s):
        for d in range(2):
            for k in range(2):
                side_ring(d, s, k, True).wait_recv()
                if across:
                    side_cross(d, s, k, True).wait_recv()
        if aligned:
            def body(d, carry):
                multiply(index(pos + (2 * d - 1) * s, 1 - core))
                return carry
            lax.fori_loop(0, 2, body, 0)

    def cross_pair(s):
        if across:
            for k in range(2):
                for d in range(2):
                    cross(d, s, k, True).wait_recv()
                    if k == d:
                        @pl.when(s == half - 1)
                        def _():
                            extra(d).start()
                    side_cross(d, s, k).start()

    side_own(True).wait_recv()
    if aligned:
        def body(d, carry):
            multiply(me + d * (1 - 2 * core))
            return carry
        lax.fori_loop(0, 2, body, 0)

    def step(s, carry):
        @pl.when(s + 1 < half)
        def _():
            forward(s + 1, 0)

        for d in range(2):
            q_hop(d, s, True).wait_recv()
            if d == 0:
                q_hop(d, s + 1).start()
            else:
                @pl.when(s < half - 1)
                def _():
                    q_hop(1, s + 1).start()
            q_side(d, s).start()

        @pl.when(s + 1 < half)
        def _():
            forward(s + 1, 1)

        cross_pair(s)
        own_pair(s)

        @pl.when(s >= 2)
        def _():
            mate_pair(s - 1)
        return carry

    lax.fori_loop(1, half, step, 0)

    q_hop(0, half, True).wait_recv()
    q_side(0, half).start()
    q_own(True).wait_recv()

    def q_wait(s, carry):
        for d in range(2):
            q_side(d, s, True).wait_recv()
        return carry

    lax.fori_loop(1, half, q_wait, 0)
    q_side(0, half, True).wait_recv()

    c_ds.wait()
    block = qtmp.shape[1]

    def unfold(b, carry):
        qtmp[...] = qall[:, pl.ds(pl.multiple_of(b * block, block), block), :].astype(jnp.float32)
        flat_ref = qtmp.reshape(members * block, LANES)
        for k in range(block):
            piece = flat_ref[pl.ds(k, members, stride=block), :]
            qmat[:, pl.ds(pl.multiple_of((b * block + k) * LANES, LANES), LANES)] = piece.astype(jnp.bfloat16)
        return carry

    lax.fori_loop(0, qall.shape[1] // block, unfold, 0)
    flat_len = qmat.shape[1]
    wide = min(flat_len, 8192)

    def score(b, total):
        cols = pl.ds(pl.multiple_of(b * wide, wide), wide)
        return total + lax.dot_general(
            qmat[:, cols], ds[:, cols], (((1,), (1,)), ((), ())), preferred_element_type=jnp.float32)

    scores = lax.fori_loop(0, flat_len // wide, score, jnp.zeros(sc.shape, jnp.float32))
    sc[...] = scores
    power = jnp.sum(scores * scores, axis=1, keepdims=True)
    lane_width = pw.shape[2]
    eye = (lax.broadcasted_iota(jnp.int32, (members, lane_width), 0)
           == lax.broadcasted_iota(jnp.int32, (members, lane_width), 1))
    pw[me] = jnp.sum(jnp.where(eye, power, 0.0), axis=0, keepdims=True)

    def p_copy(j, recv=False):
        ref = pw.at[(me - j + members) % members if recv else me]
        return remote(ref, ref, ps.at[j], pr.at[j], {"seq": (me + j) % members})

    def p_start(j, carry):
        p_copy(j).start()
        return carry

    lax.fori_loop(1, members, p_start, 0)

    mate_pair(half - 1)
    for d in range(2):
        hop(d, half, d, True).wait_recv()
        if across:
            extra(d, True).wait_recv()
        side_last(d).start()
    if aligned:
        multiply(index(pos + half, core))
    for d in range(2):
        side_last(d, True).wait_recv()
    if aligned:
        multiply(index(pos + half, 1 - core))
    else:
        def big(b, carry):
            per = LANES // shard
            weights = wf[pl.ds(b * per, per)].reshape(LANES, wf.shape[2])
            out[:, pl.ds(pl.multiple_of(b * LANES, LANES), LANES)] = lax.dot_general(
                up[...], weights, (((1,), (1,)), ((), ())), preferred_element_type=jnp.float32
            ).astype(jnp.bfloat16)
            return carry
        lax.fori_loop(0, members * shard // LANES, big, 0)

    def p_wait(j, carry):
        p_copy(j, True).wait_recv()
        return carry

    lax.fori_loop(1, members, p_wait, 0)
    summed = jnp.sum(pw[...], axis=0)
    column = jnp.sum(jnp.where(eye, summed, 0.0), axis=1, keepdims=True)
    spread = jnp.sqrt(column / (ds_h.shape[0] * members) + 1e-06)
    sc[...] = sc[...] / spread

    side_own().wait_send()
    q_own().wait_send()

    def sent(s, carry):
        for d in range(2):
            q_hop(d, s).wait_send()
            q_side(d, s).wait_send()
            for k in range(2):
                hop(d, s, k).wait_send()
                side_ring(d, s, k).wait_send()
                if across:
                    cross(d, s, k).wait_send()
                    side_cross(d, s, k).wait_send()
        return carry

    lax.fori_loop(1, half, sent, 0)
    q_hop(0, half).wait_send()
    q_side(0, half).wait_send()
    for d in range(2):
        hop(d, half, d).wait_send()
        side_last(d).wait_send()
        if across:
            extra(d).wait_send()

    def p_sent(j, carry):
        p_copy(j).wait_send()
        return carry

    lax.fori_loop(1, members, p_sent, 0)


def on_device(groups, members, *args):
    hidden, token_ids, upstream, w_value, proj_in, proj_out, in_inverse, out_inverse, datastore = args
    proj_in, proj_out = proj_in.T, jnp.swapaxes(proj_out, 1, 2)
    shard, width = w_value.shape
    tokens, model = hidden.shape
    assert token_ids.shape[0] == 1 and members % (2 * CORES) == 0
    flat = datastore.shape[1]
    across = 0
    if groups == 2:
        across = shard * 3 // 16 // 16 * 16
    half = members // CORES // 2
    steps = half + 1
    dma = pltpu.SemaphoreType.DMA
    lane_width = max(LANES, members)
    anywhere = pl.BlockSpec(memory_space=pl.ANY)
    vmem = pl.BlockSpec(memory_space=pltpu.VMEM)
    bf = jnp.bfloat16
    return pl.pallas_call(
        functools.partial(kernel, groups, members, across),
        out_shape=(
            pltpu.VMEM((tokens, members * shard), bf),
            pltpu.VMEM((members, datastore.shape[0]), jnp.float32),
        ),
        in_specs=[anywhere, anywhere, anywhere, anywhere, anywhere, anywhere, anywhere, anywhere, anywhere],
        out_specs=(vmem, vmem),
        scratch_shapes=[
            pltpu.VMEM((members, shard, width), bf),
            pltpu.VMEM((tokens, model), bf),
            pltpu.VMEM((tokens, width), bf),
            pltpu.VMEM(token_ids.shape, jnp.int32),
            pltpu.VMEM(proj_in.shape, bf),
            pltpu.VMEM(proj_out.shape, bf),
            pltpu.VMEM(in_inverse.shape, jnp.float32),
            pltpu.VMEM(out_inverse.shape, jnp.float32),
            pltpu.VMEM(datastore.shape, bf),
            pltpu.VMEM((tokens, proj_in.shape[0]), bf),
            pltpu.VMEM((members, flat // LANES, LANES), bf),
            pltpu.VMEM((members, 16, LANES), jnp.float32),
            pltpu.VMEM((members, flat), bf),
            pltpu.VMEM((members, 1, lane_width), jnp.float32),
            dma((7,)), dma((HID_CHUNKS,)), dma,
            *[dma((2, steps, 2)) for _ in range(8)], *[dma((2,)) for _ in range(4)], dma, dma,
            dma((2, steps)), dma((2, steps)), dma((2, steps)), dma((2, steps)), dma, dma,
            dma((members,)), dma((members,)),
        ],
        compiler_params=pltpu.CompilerParams(
            collective_id=0, has_side_effects=True, vmem_limit_bytes=60000 * 1024),
    )(token_ids, hidden, upstream, w_value, proj_in, proj_out, in_inverse, out_inverse, datastore)


def solution(mesh):
    rows = P(("grp", "seq"), None)
    placed = (rows, rows, rows, P("seq", None), P(), P(), P(), P(), rows)
    return jax.shard_map(
        functools.partial(on_device, mesh.shape["grp"], mesh.shape["seq"]),
        mesh=mesh,
        in_specs=placed,
        out_specs=(rows, P("grp", "seq")),
        check_vma=False,
    )
```

```python
import functools

import jax
import jax.numpy as jnp
from jax import lax
from jax.experimental import pallas as pl
from jax.experimental.pallas import tpu as pltpu
from jax.sharding import PartitionSpec as P

CORES = 2
LANES = 128
HID_CHUNKS = 4
MESH = pl.DeviceIdType.MESH


def ring_shape(chips):
    fast = 1
    while fast * fast * 4 <= chips:
        fast *= 2
    return chips // fast, fast


def chip_at(pos, chips):
    rows, cols = ring_shape(chips)
    snake = rows * (cols - 1)
    r1 = pos // (cols - 1)
    k1 = pos % (cols - 1)
    c1 = jnp.where(r1 % 2 == 0, 1 + k1, cols - 1 - k1)
    r2 = rows - 1 - (pos - snake)
    inside = pos < snake
    return jnp.where(inside, r1 * cols + c1, r2 * cols)


def pos_of(chip, chips):
    rows, cols = ring_shape(chips)
    snake = rows * (cols - 1)
    r, c = chip // cols, chip % cols
    k = jnp.where(r % 2 == 0, c - 1, cols - 1 - c)
    return jnp.where(c == 0, snake + rows - 1 - r, r * (cols - 1) + k)


def kernel(
    groups, members, pieces, share,
    tok_h, hid_h, up_h, w_h, pin_h, pout_h, ain_h, bout_h, ds_h,
    out, sc,
    wf, hid, up, tok, pin, pout, ain, bout, ds, left_s, qall, qtmp, qmat, pw,
    load_sem, hid_sem, own_sem,
    ws, wr, xs, xr, ds1, dr1, ds2, dr2, es, er, dls, dlr, dos, dor,
    qs, qr, qds, qdr, qos, qor, ps, pr,
):
    chips = members // CORES
    half = chips // 2
    shard = w_h.shape[0]
    heads, rank, head_dim = pout_h.shape
    piece = shard // pieces
    through = [[k for k in range(pieces) if k % 2 == d] for d in range(2)]
    order = [through[d] + through[1 - d] for d in range(2)]

    def width_x(d, k):
        return share[0 if k % 2 == d else 1]

    g = lax.axis_index("grp")
    me = lax.axis_index("seq")
    core = me % CORES
    pos = pos_of(me // CORES, chips)
    mate = me + 1 - 2 * core

    def index(p, c):
        return chip_at((p + 2 * chips) % chips, chips) * CORES + c

    nxt = index(pos + 1, core)
    prv = index(pos - 1, core)
    sends = (nxt, prv)

    other = mate - me

    def origins(s):
        return [index(pos - s, core), index(pos + s, core)]

    def remote(src, dst, ssem, rsem, where):
        return pltpu.make_async_remote_copy(
            src_ref=src, dst_ref=dst, send_sem=ssem, recv_sem=rsem,
            device_id=where, device_id_type=MESH)

    loads = []

    def load(src, dst, sem):
        copy = pltpu.make_async_copy(src, dst, sem)
        loads.append(copy)
        return copy

    c_w = load(w_h, wf.at[me], own_sem)
    c_tok = load(tok_h, tok, load_sem.at[0])
    c_up = load(up_h, up, load_sem.at[1])
    c_pin = load(pin_h, pin, load_sem.at[2])
    c_pout = load(pout_h, pout, load_sem.at[3])
    c_ain = load(ain_h, ain, load_sem.at[4])
    c_bout = load(bout_h, bout, load_sem.at[5])
    c_ds = load(ds_h, ds, load_sem.at[6])
    tokens = hid_h.shape[0]
    part = tokens // HID_CHUNKS
    c_hid = [load(hid_h.at[pl.ds(i * part, part)], hid.at[pl.ds(i * part, part)], hid_sem.at[i])
             for i in range(HID_CHUNKS)]
    for copy in (c_w, c_tok, c_up, c_pin, *c_hid, c_pout, c_ain, c_bout, c_ds):
        copy.start()

    barrier = pltpu.get_barrier_semaphore()

    for who in (nxt, prv, mate):
        pl.semaphore_signal(barrier, inc=1, device_id={"seq": who}, device_id_type=MESH)
    greeted = 3
    if max(share):
        pl.semaphore_signal(barrier, inc=1, device_id={"grp": 1 - g}, device_id_type=MESH)
        greeted += 1
    pl.semaphore_wait(barrier, greeted)

    def rows(o, k, off, n):
        return wf.at[o, pl.ds(pl.multiple_of(k * piece + off, 16), n)]

    def ring_rows(o, d, k):
        return rows(o, k, g * width_x(d, k), piece - width_x(d, k))

    def x_rows(o, d, k, far):
        return rows(o, k, (1 - g if far else g) * (piece - width_x(d, k)), width_x(d, k))

    def hop(d, s, k, o=0):
        ref = ring_rows(o, d, k)
        return remote(ref, ref, ws.at[d, s, k], wr.at[d, s, k], {"seq": sends[d]})

    def hop_first(d, k):
        off = pl.multiple_of(k * piece + g * width_x(d, k), 16)
        src = w_h.at[pl.ds(off, piece - width_x(d, k))]
        return remote(src, ring_rows(me, d, k), ws.at[d, 1, k], wr.at[d, 1, k], {"seq": sends[d]})

    def extra(d, k, o=0):
        ref = x_rows(o, d, k, True)
        return remote(ref, ref, es.at[k], er.at[k], {"seq": sends[d]})

    def cross(d, s, k, o=0, recv=False):
        ref = x_rows(o, d, k, recv)
        return remote(ref, ref, xs.at[d, s, k], xr.at[d, s, k], {"grp": 1 - g})

    def side_ring(d, s, k, o=0):
        ref = ring_rows(o, d, k)
        return remote(ref, ref, ds1.at[d, s, k], dr1.at[d, s, k], {"seq": mate})

    def side_cross(d, s, k, o=0):
        ref = x_rows(o, d, k, True)
        return remote(ref, ref, ds2.at[d, s, k], dr2.at[d, s, k], {"seq": mate})

    def side_last(d, k, o=0):
        ref = rows(o, k, 0, piece)
        return remote(ref, ref, dls.at[k], dlr.at[k], {"seq": mate})

    def side_own(recv=False):
        return remote(w_h, wf.at[mate if recv else me], dos, dor, {"seq": mate})

    def q_hop(d, s, o=0):
        ref = qall.at[o]
        return remote(ref, ref, qs.at[d, s], qr.at[d, s], {"seq": sends[d]})

    def q_last(d, o=0):
        part_rows = qall.shape[1] // 2
        ref = qall.at[o, pl.ds(d * part_rows, part_rows)]
        return remote(ref, ref, qs.at[d, half], qr.at[d, half], {"seq": sends[d]})

    def q_side(d, s, o=0):
        ref = qall.at[o]
        return remote(ref, ref, qds.at[d, s], qdr.at[d, s], {"seq": mate})

    def q_own(recv=False):
        ref = qall.at[mate if recv else me]
        return remote(ref, ref, qos, qor, {"seq": mate})

    for j in range(pieces):
        for d in range(2):
            hop_first(d, order[d][j]).start()
    side_own().start()

    def forward(s, j, o):
        for d in range(2):
            k = order[d][j]
            hop(d, s, k, o[d]).wait_recv()
            if k in through[d]:
                hop(d, s + 1, k, o[d]).start()
            else:
                @pl.when(s < half - 1)
                def _():
                    hop(d, s + 1, k, o[d]).start()
            if width_x(d, k):
                cross(d, s, k, o[d]).start()
            side_ring(d, s, k, o[d]).start()

    c_tok.wait()
    c_up.wait()
    live = jnp.sum((tok[...] != 0).astype(jnp.float32), axis=1, keepdims=True)
    place = lax.broadcasted_iota(jnp.int32, (tokens, 1), 0).astype(jnp.float32)
    keep = place < live
    up[...] = jnp.where(keep, up[...], jnp.zeros_like(up))
    c_pin.wait()
    for i in range(HID_CHUNKS):
        c_hid[i].wait()
        left_s[pl.ds(i * part, part), :] = lax.dot_general(
            hid[pl.ds(i * part, part), :], pin[...], (((1,), (1,)), ((), ())), preferred_element_type=jnp.float32
        ).astype(jnp.bfloat16)
    one = origins(1)
    for j in range(pieces // 2):
        forward(1, j, one)
    c_pout.wait()
    c_ain.wait()
    c_bout.wait()
    left_t = left_s[...].T
    for h in range(heads):
        right = lax.dot_general(
            up[:, h * head_dim:(h + 1) * head_dim], pout[h], (((1,), (1,)), ((), ())),
            preferred_element_type=jnp.float32
        ).astype(jnp.bfloat16)
        raw = jnp.dot(left_t, right, preferred_element_type=jnp.float32)
        inv = jnp.concatenate(
            [ain[h, pl.ds(0, rank // 2, stride=2), :], ain[h, pl.ds(1, rank // 2, stride=2), :]], axis=0)
        first = jnp.dot(inv, raw, precision=lax.Precision.HIGHEST, preferred_element_type=jnp.float32)
        both = jnp.dot(first, bout[h], precision=lax.Precision.HIGHEST, preferred_element_type=jnp.float32)
        flat = jnp.concatenate([both[:rank // 2], both[rank // 2:]], axis=1)
        qall[me, pl.ds(h * rank // 2, rank // 2), :] = flat.astype(jnp.bfloat16)

    for d in range(2):
        q_hop(d, 1, me).start()
    q_own().start()
    for j in range(pieces // 2, pieces):
        forward(1, j, one)

    aligned = shard % LANES == 0

    def multiply(o):
        cols = pl.ds(pl.multiple_of(o * shard, LANES), shard)
        out[:, cols] = lax.dot_general(
            up[...], wf[o], (((1,), (1,)), ((), ())), preferred_element_type=jnp.float32
        ).astype(jnp.bfloat16)

    def pair(o, shift):
        if aligned:
            def body(d, carry):
                multiply(jnp.where(d == 0, o[0], o[1]) + shift)
                return carry
            lax.fori_loop(0, 2, body, 0)

    def mate_pair(s, o):
        for d in range(2):
            for k in range(pieces):
                side_ring(d, s, k, o[d] + other).wait_recv()
                if width_x(d, k):
                    side_cross(d, s, k, o[d] + other).wait_recv()
        pair(o, other)

    def cross_pair(s, o):
        for j in range(pieces):
            for d in range(2):
                k = order[d][j]
                if width_x(d, k):
                    cross(d, s, k, o[d], True).wait_recv()
                    if k in through[d]:
                        @pl.when(s == half - 1)
                        def _():
                            extra(d, k, o[d]).start()
                    side_cross(d, s, k, o[d]).start()

    c_w.wait()
    side_own(True).wait_recv()
    if aligned:
        def body(d, carry):
            multiply(me + d * (1 - 2 * core))
            return carry
        lax.fori_loop(0, 2, body, 0)

    def step(s, carry):
        before, now, later = origins(s - 1), origins(s), origins(s + 1)

        @pl.when(s + 1 < half)
        def _():
            for j in range(pieces // 2):
                forward(s + 1, j, later)

        for d in range(2):
            q_hop(d, s, now[d]).wait_recv()

            @pl.when(s < half - 1)
            def _():
                q_hop(d, s + 1, now[d]).start()

            @pl.when(s == half - 1)
            def _():
                q_last(d, now[d]).start()

            q_side(d, s, now[d]).start()

        @pl.when(s + 1 < half)
        def _():
            for j in range(pieces // 2, pieces):
                forward(s + 1, j, later)

        cross_pair(s, now)
        pair(now, 0)

        @pl.when(s >= 2)
        def _():
            mate_pair(s - 1, before)
        return carry

    lax.fori_loop(1, half, step, 0)

    end = index(pos + half, core)
    for d in range(2):
        q_last(d, end).wait_recv()
    q_side(0, half, end).start()
    q_own(True).wait_recv()

    def q_wait(s, carry):
        o = origins(s)
        for d in range(2):
            q_side(d, s, o[d] + other).wait_recv()
        return carry

    lax.fori_loop(1, half, q_wait, 0)
    q_side(0, half, end + other).wait_recv()

    c_ds.wait()
    block = qtmp.shape[1]

    def unfold(b, carry):
        qtmp[...] = qall[:, pl.ds(pl.multiple_of(b * block, block), block), :].astype(jnp.float32)
        flat_ref = qtmp.reshape(members * block, LANES)
        for k in range(block):
            piece = flat_ref[pl.ds(k, members, stride=block), :]
            qmat[:, pl.ds(pl.multiple_of((b * block + k) * LANES, LANES), LANES)] = piece.astype(jnp.bfloat16)
        return carry

    lax.fori_loop(0, qall.shape[1] // block, unfold, 0)
    flat_len = qmat.shape[1]
    wide = min(flat_len, 8192)

    def score(b, total):
        cols = pl.ds(pl.multiple_of(b * wide, wide), wide)
        return total + lax.dot_general(
            qmat[:, cols], ds[:, cols], (((1,), (1,)), ((), ())), preferred_element_type=jnp.float32)

    scores = lax.fori_loop(0, flat_len // wide, score, jnp.zeros(sc.shape, jnp.float32))
    sc[...] = scores
    power = jnp.sum(scores * scores, axis=1, keepdims=True)
    lane_width = pw.shape[2]
    eye = (lax.broadcasted_iota(jnp.int32, (members, lane_width), 0)
           == lax.broadcasted_iota(jnp.int32, (members, lane_width), 1))
    pw[me] = jnp.sum(jnp.where(eye, power, 0.0), axis=0, keepdims=True)

    def p_copy(j, recv=False):
        ref = pw.at[(me - j + members) % members if recv else me]
        return remote(ref, ref, ps.at[j], pr.at[j], {"seq": (me + j) % members})

    def p_start(j, carry):
        p_copy(j).start()
        return carry

    lax.fori_loop(1, members, p_start, 0)

    mate_pair(half - 1, origins(half - 1))
    for j in range(pieces // 2):
        for d in range(2):
            k = order[d][j]
            hop(d, half, k, end).wait_recv()
            if width_x(d, k):
                extra(d, k, end).wait_recv()
            side_last(d, k, end).start()
    if aligned:
        multiply(end)
    for d in range(2):
        for k in through[d]:
            side_last(d, k, end + other).wait_recv()
    if aligned:
        multiply(end + other)
    else:
        def big(b, carry):
            per = LANES // shard
            weights = wf[pl.ds(b * per, per)].reshape(LANES, wf.shape[2])
            out[:, pl.ds(pl.multiple_of(b * LANES, LANES), LANES)] = lax.dot_general(
                up[...], weights, (((1,), (1,)), ((), ())), preferred_element_type=jnp.float32
            ).astype(jnp.bfloat16)
            return carry
        lax.fori_loop(0, members * shard // LANES, big, 0)

    def p_wait(j, carry):
        p_copy(j, True).wait_recv()
        return carry

    lax.fori_loop(1, members, p_wait, 0)
    summed = jnp.sum(pw[...], axis=0)
    column = jnp.sum(jnp.where(eye, summed, 0.0), axis=1, keepdims=True)
    spread = jnp.sqrt(column / (ds_h.shape[0] * members) + 1e-06)
    sc[...] = sc[...] / spread

    side_own().wait_send()
    q_own().wait_send()

    def sent(s, carry):
        for d in range(2):
            q_hop(d, s).wait_send()
            q_side(d, s).wait_send()
            for k in range(pieces):
                hop(d, s, k).wait_send()
                side_ring(d, s, k).wait_send()
                if width_x(d, k):
                    cross(d, s, k).wait_send()
                    side_cross(d, s, k).wait_send()
        return carry

    lax.fori_loop(1, half, sent, 0)
    q_side(0, half).wait_send()
    for d in range(2):
        q_last(d).wait_send()
        for k in through[d]:
            hop(d, half, k).wait_send()
            side_last(d, k).wait_send()
            if width_x(d, k):
                extra(d, k).wait_send()

    def p_sent(j, carry):
        p_copy(j).wait_send()
        return carry

    lax.fori_loop(1, members, p_sent, 0)


def on_device(groups, members, *args):
    hidden, token_ids, upstream, w_value, proj_in, proj_out, in_inverse, out_inverse, datastore = args
    proj_in, proj_out = proj_in.T, jnp.swapaxes(proj_out, 1, 2)
    shard, width = w_value.shape
    tokens, model = hidden.shape
    assert token_ids.shape[0] == 1 and members % (2 * CORES) == 0
    flat = datastore.shape[1]
    pieces = min(2, shard // 16)
    piece = shard // pieces
    share = (0, 0)
    if groups == 2:
        share = (piece * 3 // 8 // 16 * 16,) * 2
    half = members // CORES // 2
    steps = half + 1
    dma = pltpu.SemaphoreType.DMA
    lane_width = max(LANES, members)
    anywhere = pl.BlockSpec(memory_space=pl.ANY)
    vmem = pl.BlockSpec(memory_space=pltpu.VMEM)
    bf = jnp.bfloat16
    return pl.pallas_call(
        functools.partial(kernel, groups, members, pieces, share),
        out_shape=(
            pltpu.VMEM((tokens, members * shard), bf),
            pltpu.VMEM((members, datastore.shape[0]), jnp.float32),
        ),
        in_specs=[anywhere, anywhere, anywhere, anywhere, anywhere, anywhere, anywhere, anywhere, anywhere],
        out_specs=(vmem, vmem),
        scratch_shapes=[
            pltpu.VMEM((members, shard, width), bf),
            pltpu.VMEM((tokens, model), bf),
            pltpu.VMEM((tokens, width), bf),
            pltpu.VMEM(token_ids.shape, jnp.int32),
            pltpu.VMEM(proj_in.shape, bf),
            pltpu.VMEM(proj_out.shape, bf),
            pltpu.VMEM(in_inverse.shape, jnp.float32),
            pltpu.VMEM(out_inverse.shape, jnp.float32),
            pltpu.VMEM(datastore.shape, bf),
            pltpu.VMEM((tokens, proj_in.shape[0]), bf),
            pltpu.VMEM((members, flat // LANES, LANES), bf),
            pltpu.VMEM((members, 16, LANES), jnp.float32),
            pltpu.VMEM((members, flat), bf),
            pltpu.VMEM((members, 1, lane_width), jnp.float32),
            dma((7,)), dma((HID_CHUNKS,)), dma,
            *[dma((2, steps, pieces)) for _ in range(8)], *[dma((pieces,)) for _ in range(4)], dma, dma,
            dma((2, steps)), dma((2, steps)), dma((2, steps)), dma((2, steps)), dma, dma,
            dma((members,)), dma((members,)),
        ],
        compiler_params=pltpu.CompilerParams(
            collective_id=0, has_side_effects=True, vmem_limit_bytes=60000 * 1024),
    )(token_ids, hidden, upstream, w_value, proj_in, proj_out, in_inverse, out_inverse, datastore)


def solution(mesh):
    rows = P(("grp", "seq"), None)
    placed = (rows, rows, rows, P("seq", None), P(), P(), P(), P(), rows)
    return jax.shard_map(
        functools.partial(on_device, mesh.shape["grp"], mesh.shape["seq"]),
        mesh=mesh,
        in_specs=placed,
        out_specs=(rows, P("grp", "seq")),
        check_vma=False,
    )
```
